32 devices in a mesh: groups: 2 (over y), people: 4 (over z), blocks: 2 (over x), sub: 2 (over core).
Axes of the slice: x: 2, y: 2, z: 4, core: 2. Of those that a mesh axis runs over, the one named last changes fastest.
Arguments:
- dosage: int32 [4096, 2048], P(('groups', 'people', 'sub'), 'blocks'), parts along dimension 0, may hold values from 0 to 200
- fold: int32 [4096], P(('groups', 'people', 'sub')), parts along dimension 0, may hold values from 0 to 1, as said below
- pheno: bfloat16 [4096, 48], P(('groups', 'people', 'sub')), parts along dimension 0, may hold values from -8 to 8
- ridges: float32 [5], replicated, may hold values from 1 to 20
Outputs:
- second: float32 [48, 5, 4096], P(('blocks', 'sub'), None, ('groups', 'people')), parts along dimension 2
The draws below stay inside these ranges and needn't reach their ends.
There are 2 independent parts, one for each index of `groups`. The reference program is written for one: setup_inputs(seed, part) draws one part's arguments, and reference() takes and returns one part's arrays. A program takes and returns all parts, laid end to end along the dimension named above; an argument that names none is the same for every part. Nothing has to cross between parts.
Inputs may be any that keep to these rules, and one draw needn't show every extreme that they name: Each fold holds exactly 1024 people.
All inputs are finite; a program needn't handle non-finite values.
Results may differ from the reference program's by a relative error of at most 0.0021.
Values may be sent and summed in bfloat16 or wider, within the bound.
No kernel may reach another device: no remote copies, remote signals or barrier semaphores. Data moves between devices by JAX's collectives and lax.ppermute only.
A program may use at most 64 MiB of HBM per device.

```python
import math
import jax
import jax.numpy as jnp
from jax import lax

BLOCK = 1024
TRAITS = 48
RIDGES = 5
FOLDS = 2
ITERS = 10
ITERS_TWO = 4
PEOPLE = 2048
NBLK = 2
VARIANTS = 2048


def dosage_table(key):
    level_key = jax.random.fold_in(key, 71)
    value_key = jax.random.fold_in(key, 73)
    levels = jax.random.randint(level_key, (VARIANTS,), 1, 41)
    levels = levels.at[:5].set(40)
    offsets = (40 - levels) // 2
    values = jax.random.randint(value_key, (PEOPLE, VARIANTS), 0, levels[None, :] + 1) + offsets[None, :]
    values = values.at[0, :5].set(40)
    values = values.at[1, :5].set(0)
    summed = values
    for shift_step in range(1, 5):
        summed = summed + jnp.roll(values, -shift_step, axis=1)
    return summed.astype(jnp.int32)


def draw_dosage(key, part):
    return dosage_table(key)


def draw_fold(key, part):
    order = jax.random.permutation(jax.random.fold_in(key, 31), PEOPLE)
    return (order % FOLDS).astype(jnp.int32)


def draw_pheno(key, part):
    centred = dosage_table(key).astype(jnp.float32) - 100.0
    effects = jax.random.normal(jax.random.fold_in(key, 11), (VARIANTS, TRAITS), jnp.float32)
    signal = jnp.dot(centred, effects)
    signal = (signal - jnp.mean(signal, 0)) / (jnp.std(signal, 0) + 1e-06)
    noise = jax.random.normal(jax.random.fold_in(key, 13), (PEOPLE, TRAITS), jnp.float32)
    heritable = jax.random.uniform(jax.random.fold_in(key, 17), (TRAITS,), jnp.float32, 0.2, 0.8)
    values = jnp.sqrt(heritable) * signal + jnp.sqrt(1.0 - heritable) * noise
    return jnp.clip(values, -8.0, 8.0).astype(jnp.bfloat16)


def setup_inputs(seed: int = 0, part: int = 0) -> dict:
    arg_keys = jax.random.split(jax.random.key(seed), 5)
    own_keys = jax.random.split(jax.random.fold_in(arg_keys[4], part), 5)
    dosage = draw_dosage(jax.random.fold_in(jax.random.fold_in(arg_keys[4], part), 71), part)
    fold = draw_fold(jax.random.fold_in(jax.random.fold_in(arg_keys[4], part), 71), part)
    pheno = draw_pheno(jax.random.fold_in(jax.random.fold_in(arg_keys[4], part), 71), part)
    ridges = jnp.clip(jnp.exp(jax.random.uniform(arg_keys[3], (RIDGES,), jnp.float32, math.log(1.0), math.log(20.0))), 1.0, 20.0)
    return dict(dosage=dosage, fold=fold, pheno=pheno, ridges=ridges)


highest = lax.Precision.HIGHEST

def conjugate(apply_system, right_side, steps):
    estimate = jnp.zeros_like(right_side)
    residual = right_side
    direction = right_side
    current = lax.optimization_barrier(jnp.sum(residual * residual, -2, keepdims=True))
    for step in range(steps):
        image = apply_system(direction)
        alpha = current / lax.optimization_barrier(jnp.sum(direction * image, -2, keepdims=True))
        estimate = estimate + alpha * direction
        residual = residual - alpha * image
        following = lax.optimization_barrier(jnp.sum(residual * residual, -2, keepdims=True))
        direction = residual + following / current * direction
        current = following
    return estimate

def covariance_rows(gram_rows, row_sums, all_sums, row_mean, all_mean, train_count):
    return gram_rows - row_sums[:, None] * all_mean[None, :] - row_mean[:, None] * all_sums[None, :] + train_count * row_mean[:, None] * all_mean[None, :]

def train_total(pieces, fold_index):
    return sum([pieces[other] for other in range(FOLDS) if other != fold_index])

def reference(dosage, fold, pheno, ridges):
    people = dosage.shape[0]
    train_count = people - people // FOLDS
    centred = (dosage - 100).astype(jnp.bfloat16)
    pheno_wide = pheno.astype(jnp.float32)
    masks = [fold[:, None] == fold_index for fold_index in range(FOLDS)]
    level_zero = []
    for block_index in range(NBLK):
        section = centred[:, block_index * BLOCK:(block_index + 1) * BLOCK]
        grams, sums, squares, cross, totals = ([], [], [], [], [])
        for mask in masks:
            masked = jnp.where(mask, section, jnp.zeros_like(section))
            grams.append(jnp.dot(masked.T, section, preferred_element_type=jnp.float32))
            masked_wide = masked.astype(jnp.float32)
            sums.append(lax.optimization_barrier(jnp.sum(masked_wide, 0)))
            squares.append(lax.optimization_barrier(jnp.sum(masked_wide * masked_wide, 0)))
            cross.append(jnp.dot(masked.T, pheno, preferred_element_type=jnp.float32))
            totals.append(lax.optimization_barrier(jnp.sum(jnp.where(mask, pheno_wide, 0.0), 0)))
        column_mean = sum(sums) / people
        column_spread = jnp.sqrt(sum(squares) / people - column_mean * column_mean + 1e-05)
        shifts = jnp.repeat(ridges, TRAITS)
        prediction = jnp.zeros((people, RIDGES * TRAITS), jnp.float32)
        for fold_index in range(FOLDS):
            sums_train = train_total(sums, fold_index)
            covariance = covariance_rows(train_total(grams, fold_index), sums_train, sums_train, column_mean, column_mean, train_count)
            system = covariance / (train_count * column_spread[:, None] * column_spread[None, :])
            right_side = (train_total(cross, fold_index) - column_mean[:, None] * train_total(totals, fold_index)[None, :]) / (train_count * column_spread[:, None])
            estimate = conjugate(lambda direction: jnp.dot(system, direction, precision=highest) + shifts * direction, jnp.tile(right_side, (1, RIDGES)), ITERS)
            scaled = (estimate / column_spread[:, None]).astype(jnp.bfloat16)
            offset = jnp.dot(column_mean, scaled.astype(jnp.float32), precision=highest)
            outcome = jnp.dot(section, scaled, preferred_element_type=jnp.float32) - offset
            prediction = prediction + jnp.where(masks[fold_index], outcome, 0.0)
        level_zero.append(prediction.astype(jnp.bfloat16).reshape(people, RIDGES, TRAITS))
    stacked = jnp.stack(level_zero, 1)
    predictors = jnp.transpose(stacked, (0, 3, 1, 2)).reshape(people, TRAITS, NBLK * RIDGES)
    predictors_wide = predictors.astype(jnp.float32)
    gram_two = jnp.einsum('nta,ntb->tab', predictors_wide, predictors_wide, precision=highest) / people
    cross_two = jnp.einsum('nt,nta->ta', pheno_wide, predictors_wide, precision=highest) / people
    level = jnp.trace(gram_two, axis1=1, axis2=2) / (NBLK * RIDGES) + 1e-06
    level_shift = ridges[None, None, :] * level[:, None, None]
    right_two = jnp.broadcast_to(cross_two[:, :, None], (TRAITS, NBLK * RIDGES, RIDGES))
    weights = conjugate(lambda direction: jnp.einsum('tab,tbr->tar', gram_two, direction, precision=highest) + level_shift * direction, right_two, ITERS_TWO)
    return jnp.einsum('nta,tar->trn', predictors_wide, weights, precision=highest)
```

```python
import functools

import jax
import jax.numpy as jnp
from jax import lax
from jax.experimental import pallas as pl
from jax.experimental.pallas import tpu as pltpu
from jax.sharding import PartitionSpec as P

TRAITS = 48
RIDGES = 5
FOLDS = 2
ITERS = 10
ITERS_TWO = 4

f32 = jnp.float32
bf16 = jnp.bfloat16
highest = lax.Precision.HIGHEST
natural = (((1,), (0,)), ((), ()))
transposed = (((1,), (1,)), ((), ()))


def round_up(value, step):
    return -(-value // step) * step


def split_high_low(value):
    high = value.astype(bf16)
    return high, (value - high.astype(f32)).astype(bf16)


def iota(shape, axis):
    return lax.broadcasted_iota(jnp.int32, shape, axis)


def count_steps(index, step, most):
    return sum([(index >= step * (turn + 1)).astype(jnp.int32) for turn in range(most)])


def pack_kernel(dosage_ref, fold_ref, pheno_ref, packed_ref, tail_ref):
    row_count, block_size = dosage_ref.shape
    trait_count = pheno_ref.shape[0]
    centred = (dosage_ref[...] - 100).astype(f32)
    packed_ref[:block_size, :] = centred.T.astype(bf16)
    packed_ref[block_size : block_size + trait_count, :] = pheno_ref[...]
    tail_ref[...] = jnp.zeros_like(tail_ref)
    tail_ref[0:1, :] = fold_ref[...].astype(f32)
    rest = jnp.sum(centred * centred, 0, keepdims=True)
    place = 1
    for piece in range(3):
        part = rest.astype(bf16).astype(f32)
        rest = rest - part
        for start in range(0, block_size, row_count):
            tail_ref[place : place + 1, :] = part[:, start : start + row_count]
            place += 1
    packed_ref[block_size + trait_count :, :] = tail_ref[...].astype(bf16)


def fold_sign(place, first_host, host_count):
    if host_count != 2:
        return 1
    return jnp.where(place <= first_host, 1, -1)


def quarter_of(turn, place, first_host, host_count, people_count):
    return lax.rem(
        place + fold_sign(place, first_host, host_count) * turn + people_count, people_count
    )


def start_copies(chunks, people_ref, sems, starts):
    copies = []
    for index, (chunk, start) in enumerate(zip(chunks, starts)):
        width = chunk.shape[1]
        copies.append(
            pltpu.make_async_copy(
                chunk,
                people_ref.at[:, pl.ds(pl.multiple_of(start, width), width)],
                sems.at[index],
            )
        )
    for copy in copies:
        copy.start()
    return copies


def base_traits(quarter, part_rows, host, trait_group):
    row = iota((2 * part_rows, TRAITS), 0)
    part = (row >= part_rows).astype(jnp.int32)
    place = row - part_rows * part
    place = place - quarter * count_steps(place, quarter, -(-part_rows // quarter))
    return place + quarter * part + host * trait_group


def masked_targets(people_ref, block_size, lanes, core, choose):
    own = people_ref[block_size + TRAITS :, lanes].astype(f32)[0:1, :] == core.astype(f32)
    train = jnp.where(own, 0.0, 1.0)
    targets = lax.dot_general(
        choose,
        people_ref[block_size : block_size + TRAITS, lanes],
        natural,
        preferred_element_type=f32,
    )
    return targets * train, train


def fill_left(people_ref, left_ref, block_size, lanes, core, choose):
    targets, train = masked_targets(people_ref, block_size, lanes, core, choose)
    width = train.shape[1]
    left_ref[:block_size, :] = people_ref[:block_size, lanes] * train.astype(bf16)
    rows = targets.shape[0]
    left_ref[block_size : block_size + rows, :] = targets.astype(bf16)
    left_ref[block_size + rows :, :] = jnp.where(iota((16, width), 0) == 0, train, 1.0).astype(
        bf16
    )


def left_slabs(total):
    half = round_up(total // 2, 16)
    return [(0, half), (half, total)]


def early_kernel(sizes, *refs):
    block_size, row_count, trait_group, quarter, part_rows, first_host, host_count, _ = sizes
    chunks, (gram_ref, pheno_ref, people_ref, left_ref, sems) = refs[:4], refs[4:]
    core = lax.axis_index("sub")
    host = jnp.clip(lax.axis_index("people") - first_host, 0, host_count - 1)
    starts = [
        (2 * turn + (core if side == 0 else 1 - core)) * row_count
        for turn in range(2)
        for side in range(2)
    ]
    copies = start_copies(chunks, people_ref, sems, starts)
    for copy in copies:
        copy.wait()
    choose = (
        iota((2 * part_rows, TRAITS), 1) == base_traits(quarter, part_rows, host, trait_group)
    ).astype(bf16)
    fill_left(people_ref, left_ref, block_size, slice(None), core, choose)
    for start, stop in left_slabs(left_ref.shape[0]):
        gram_ref[start:stop, :] = lax.dot_general(
            left_ref[start:stop, :],
            people_ref[:block_size, :],
            transposed,
            preferred_element_type=f32,
        )
    first = lax.axis_index("blocks") * (2 * quarter) + core * quarter
    pick = iota((16, TRAITS), 1) == iota((16, TRAITS), 0) + first
    pheno_ref[...] = lax.dot_general(
        pick.astype(bf16),
        people_ref[block_size : block_size + TRAITS, : 2 * row_count],
        natural,
        preferred_element_type=f32,
    ).astype(bf16)


def fit_kernel(sizes, rows, ridges_ref, early_ref, *refs):
    (
        block_size, row_count, trait_group, quarter, part_rows, first_host, host_count, people_count,
    ) = sizes
    chunk_count = people_count * 2
    chunks = refs[:chunk_count]
    keep_ref, send_ref = refs[chunk_count : chunk_count + 2]
    (
        people_ref,
        left_ref,
        gram_ref,
        high_ref,
        low_ref,
        column_ref,
        history_ref,
        direction_ref,
        split_ref,
        alpha_ref,
        beta_ref,
        tall_ref,
        predict_ref,
        sems,
        early_sem,
    ) = refs[chunk_count + 2 :]
    core = lax.axis_index("sub")
    place = lax.axis_index("people")
    host = jnp.clip(place - first_host, 0, host_count - 1)
    people = chunk_count * row_count
    train_count = people - people // FOLDS
    width = 2 * row_count
    base_rows = 2 * part_rows
    starts = []
    for turn in range(people_count):
        where = quarter_of(turn, place, first_host, host_count, people_count)
        for side in range(2):
            starts.append(where * width + (core if side == 0 else 1 - core) * row_count)
    early_copy = pltpu.make_async_copy(early_ref, gram_ref, early_sem)
    early_copy.start()
    copies = start_copies(chunks, people_ref, sems, starts)
    for copy in copies[2 : chunk_count - 2]:
        copy.wait()
    choose = (
        iota((base_rows, TRAITS), 1) == base_traits(quarter, part_rows, host, trait_group)
    ).astype(bf16)
    early_copy.wait()

    def late(turn, carry):
        where = quarter_of(turn, place, first_host, host_count, people_count)
        lanes = pl.ds(pl.multiple_of(where * width, width), width)
        fill_left(people_ref, left_ref, block_size, lanes, core, choose)
        for start, stop in left_slabs(left_ref.shape[0]):
            gram_ref[start:stop, :] += lax.dot_general(
                left_ref[start:stop, :],
                people_ref[:block_size, lanes],
                transposed,
                preferred_element_type=f32,
            )
        return carry

    lax.fori_loop(1, people_count - 1, late, 0, unroll=people_count <= 4)
    for copy in copies[:2] + copies[chunk_count - 2 :]:
        copy.wait()

    tail = people_ref[block_size + TRAITS :, :].astype(f32)
    own = tail[0:1, :] == core.astype(f32)
    square_parts = []
    pieces_per = block_size // row_count
    for piece in range(pieces_per):
        part = jnp.zeros((1, row_count), f32)
        for chunk in range(chunk_count):
            lanes = slice(chunk * row_count, (chunk + 1) * row_count)
            for level in range(3):
                line = 1 + level * pieces_per + piece
                part = part + tail[line : line + 1, lanes]
        square_parts.append(part)
    squares = jnp.concatenate(square_parts, 1)
    targets, _ = masked_targets(people_ref, block_size, slice(None), core, choose)
    totals = jnp.sum(targets, 1, keepdims=True)
    train_sums = gram_ref[block_size + base_rows : block_size + base_rows + 1, :]
    mean = gram_ref[block_size + base_rows + 1 : block_size + base_rows + 2, :] / people
    spread = jnp.sqrt(squares / people - mean * mean + 1e-05)
    inverse = 1.0 / spread
    offset_sums = train_sums - (0.5 * train_count) * mean
    shares = inverse * (1.0 / train_count)
    column_ref[...] = jnp.concatenate([mean, offset_sums, shares] + [mean] * 5, 0).T

    slab = 64

    def assemble(turn, carry):
        span = pl.ds(pl.multiple_of(turn * slab, slab), slab)
        columns = column_ref[span, :]
        system = (
            (gram_ref[span, :] - columns[:, 1:2] * mean - columns[:, 0:1] * offset_sums)
            * columns[:, 2:3]
            * inverse
        )
        high, low = split_high_low(system)
        high_ref[span, :] = high
        low_ref[span, :] = low
        return carry

    lax.fori_loop(0, block_size // slab, assemble, 0)

    right = (gram_ref[block_size : block_size + base_rows, :] - totals * mean) * shares
    smallest = ridges_ref[0]
    for ridge in range(1, RIDGES):
        smallest = jnp.minimum(smallest, ridges_ref[ridge])
    history_ref[:base_rows, :] = right
    direction_ref[...] = right
    high, low = split_high_low(right)
    split_ref[:base_rows, :] = high
    split_ref[base_rows:, :] = low

    def step(turn, current):
        both = lax.dot_general(
            split_ref[...], high_ref[...], natural, preferred_element_type=f32
        )
        other = lax.dot_general(
            split_ref[:base_rows, :], low_ref[...], natural, preferred_element_type=f32
        )
        direction = direction_ref[...]
        image = both[:base_rows, :] + (both[base_rows:, :] + other) + smallest * direction
        alpha = current / jnp.sum(direction * image, 1, keepdims=True)
        residual = (
            history_ref[pl.ds(pl.multiple_of(turn * base_rows, base_rows), base_rows), :]
            - alpha * image
        )
        following = jnp.sum(residual * residual, 1, keepdims=True)
        beta = following / current
        direction = residual + beta * direction
        history_ref[
            pl.ds(pl.multiple_of((turn + 1) * base_rows, base_rows), base_rows), :
        ] = residual
        direction_ref[...] = direction
        high, low = split_high_low(direction)
        split_ref[:base_rows, :] = high
        split_ref[base_rows:, :] = low
        alpha_ref[pl.ds(pl.multiple_of(turn * base_rows, base_rows), base_rows), :] = alpha
        beta_ref[pl.ds(pl.multiple_of(turn * base_rows, base_rows), base_rows), :] = beta
        return following

    lax.fori_loop(0, ITERS, step, jnp.sum(right * right, 1, keepdims=True))

    lane = iota((1, 128), 1)
    extra = jnp.zeros((1, 128), f32)
    for ridge in range(RIDGES):
        extra = jnp.where(lane == ridge, ridges_ref[ridge] - smallest, extra)
    ratio = jnp.ones((base_rows, 128), f32)
    scale = ratio
    link = jnp.zeros((base_rows, 1), f32)
    scales, alphas, betas = [], [], []
    for turn in range(ITERS):
        span = slice(turn * base_rows, (turn + 1) * base_rows)
        alpha, beta = alpha_ref[span, :], beta_ref[span, :]
        ratio = 1.0 / (1.0 + extra * alpha + (alpha * link) * (1.0 - ratio))
        scales.append(scale)
        alphas.append(alpha * ratio)
        betas.append(beta * ratio * ratio)
        scale = scale * ratio
        link = beta / alpha
    reach = alphas[-1]
    factors = [scales[-1] * reach]
    for turn in range(ITERS - 2, -1, -1):
        reach = alphas[turn] + betas[turn] * reach
        factors.append(scales[turn] * reach)
    factors = factors[::-1]
    for ridge in range(RIDGES):
        for start in range(0, base_rows, 16):
            fit = jnp.zeros((16, block_size), f32)
            for turn in range(ITERS):
                line = turn * base_rows + start
                fit = (
                    fit
                    + factors[turn][start : start + 16, ridge : ridge + 1]
                    * history_ref[line : line + 16, :]
                )
            line = ridge * base_rows + start
            tall_ref[line : line + 16, :] = (fit * inverse).astype(bf16)

    tall_count = RIDGES * base_rows
    row = iota((2 * rows, tall_count), 0)
    part = (row >= rows).astype(jnp.int32)
    line = row - rows * part
    ridge = jnp.minimum(count_steps(line, quarter, RIDGES), RIDGES - 1)
    source = ridge * base_rows + part * part_rows + (line - quarter * ridge)
    source = jnp.where(line < quarter * RIDGES, source, 0)
    pack = (iota((2 * rows, tall_count), 1) == source).astype(bf16)
    scaled = lax.dot_general(pack, tall_ref[...], natural, preferred_element_type=f32)
    offset = jnp.sum(scaled * mean, 1, keepdims=True)
    scaled = scaled.astype(bf16)

    def predict(lanes, own):
        outcome = lax.dot_general(
            scaled, people_ref[:block_size, lanes], natural, preferred_element_type=f32
        )
        predict_ref[:, lanes] = jnp.where(own, outcome - offset, 0.0).astype(bf16)

    if people_count <= 4:
        predict(slice(None), own)
    else:

        def predict_part(turn, carry):
            lanes = pl.ds(pl.multiple_of(turn * width, width), width)
            lines = people_ref[block_size + TRAITS :, lanes].astype(f32)
            predict(lanes, lines[0:1, :] == core.astype(f32))
            return carry

        lax.fori_loop(0, people_count, predict_part, 0)
    keep_ref[...] = predict_ref[pl.ds(pl.multiple_of(core * rows, rows), rows), :]
    send_ref[...] = predict_ref[pl.ds(pl.multiple_of((1 - core) * rows, rows), rows), :]


def join_kernel(sizes, keep_ref, received_ref, *piece_refs):
    first_host, host_count, people_count = sizes
    place = lax.axis_index("people")
    width = piece_refs[0].shape[1]
    for turn, piece_ref in enumerate(piece_refs):
        where = quarter_of(turn, place, first_host, host_count, people_count)
        lanes = pl.ds(pl.multiple_of(where * width, width), width)
        piece_ref[...] = (
            keep_ref[:, lanes].astype(f32) + received_ref[:, lanes].astype(f32)
        ).astype(bf16)


def split_index(index, quarter, rows, block_count):
    block = count_steps(index, rows, block_count - 1)
    place = index - rows * block
    ridge = count_steps(place, quarter, RIDGES)
    return block * RIDGES + ridge, place - quarter * ridge, ridge < RIDGES


def moment_kernel(sizes, pheno_ref, *refs):
    quarter, rows, block_count, stat_rows = sizes
    pieces, sums_ref = refs[:-1], refs[-1]
    width = block_count * rows
    predictors = jnp.concatenate([piece[...] for piece in pieces], 0)
    slot, trait, live = split_index(iota((1, width), 1), quarter, rows, block_count)
    _, row_trait, row_live = split_index(iota((width, 1), 0), quarter, rows, block_count)
    gram = lax.dot_general(predictors, predictors, transposed, preferred_element_type=f32)
    gram = jnp.where((row_trait == trait) & row_live & live, gram, 0.0)
    pick = (iota((stat_rows, width), 0) == slot) & live
    table = lax.dot_general(
        pick.astype(f32), gram, natural, precision=highest, preferred_element_type=f32
    )
    cross = lax.dot_general(pheno_ref[...], predictors, transposed, preferred_element_type=f32)
    chosen = (iota((16, width), 0) == trait) & live
    cross = jnp.sum(jnp.where(chosen, cross, 0.0), 0, keepdims=True)
    sums_ref[...] = jnp.where(iota((stat_rows, width), 0) == stat_rows - 1, cross, table)


def second_kernel(sizes, ridges_ref, *refs):
    people, quarter, rows, block_count, stat_rows, part_count = sizes
    parts = refs[:part_count]
    pieces = refs[part_count : part_count + block_count]
    out_ref = refs[-1]
    width = block_count * rows
    slots = block_count * RIDGES
    table = parts[0][...]
    for part in parts[1:]:
        table = table + part[...]
    table = table * (1.0 / people)
    slot, trait, live = split_index(iota((1, width), 1), quarter, rows, block_count)
    _, row_trait, row_live = split_index(iota((width, 1), 0), quarter, rows, block_count)
    out_lane = iota((1, 128), 1)
    out_ridge = count_steps(out_lane, 16, 7)
    out_trait = out_lane - 16 * out_ridge
    out_live = (out_trait < quarter) & (out_ridge < RIDGES)
    expand = ((row_trait == out_trait) & row_live & out_live).astype(f32)
    stacked = jnp.concatenate(
        [jnp.where((slot == index) & live, table, 0.0) for index in range(slots)], 0
    )
    wide = lax.dot_general(
        stacked, expand, natural, precision=highest, preferred_element_type=f32
    )
    sublane = iota((stat_rows, 128), 0)
    columns = []
    residual = jnp.zeros((stat_rows, 128), f32)
    trace = jnp.zeros((stat_rows, 128), f32)
    for index in range(slots):
        column = wide[index * stat_rows : (index + 1) * stat_rows, :]
        here = sublane == index
        residual = jnp.where(here, column[stat_rows - 1 : stat_rows, :], residual)
        column = jnp.where(sublane < slots, column, 0.0)
        trace = jnp.where(here, column, trace)
        columns.append(column)
    level = jnp.sum(trace, 0, keepdims=True) / slots + 1e-06
    ridge = jnp.zeros((1, 128), f32)
    for index in range(RIDGES):
        ridge = jnp.where(out_ridge == index, ridges_ref[index], ridge)
    level_shift = ridge * level
    direction = residual
    weights = jnp.zeros_like(residual)
    current = jnp.sum(residual * residual, 0, keepdims=True)
    for step in range(ITERS_TWO):
        image = level_shift * direction
        for index in range(slots):
            image = image + columns[index] * direction[index : index + 1, :]
        alpha = current / jnp.sum(direction * image, 0, keepdims=True)
        weights = weights + alpha * direction
        residual = residual - alpha * image
        following = jnp.sum(residual * residual, 0, keepdims=True)
        direction = residual + following / current * direction
        current = following
    weights = jnp.where(out_live, weights, 0.0)
    turned = weights.T
    pick = (iota((stat_rows, width), 0) == slot) & live
    tall = lax.dot_general(
        turned, pick.astype(f32), natural, precision=highest, preferred_element_type=f32
    )
    row = iota((128, 1), 0)
    tall = jnp.where(row - 16 * count_steps(row, 16, 7) == trait, tall, 0.0)
    tall = tall[: RIDGES * 16, :]
    high, low = split_high_low(tall)
    predictors = jnp.concatenate([piece[...] for piece in pieces], 0)
    both = lax.dot_general(
        jnp.concatenate([high, low], 0), predictors, natural, preferred_element_type=f32
    )
    answer = both[: RIDGES * 16, :] + both[RIDGES * 16 :, :]
    for ridge in range(RIDGES):
        out_ref[ridge] = answer[ridge * 16 : ridge * 16 + quarter, :]


def whole(count):
    return [pl.BlockSpec(memory_space=pltpu.VMEM)] * count


def anywhere(count):
    return [pl.BlockSpec(memory_space=pl.ANY)] * count


def shards(dosage, fold, pheno, ridges):
    row_count, block_size = dosage.shape
    people_count = lax.axis_size("people")
    block_count = lax.axis_size("blocks")
    people = row_count * people_count * 2
    host_count = block_count
    first_host = people_count // 2 - host_count // 2
    hosts = [first_host + host for host in range(host_count)]
    trait_group = TRAITS // host_count
    quarter = trait_group // 2
    rows = round_up(quarter * RIDGES, 16)
    part_rows = round_up(quarter, 16)
    base_rows = 2 * part_rows
    tail_rows = round_up(1 + 3 * (block_size // row_count), 16)
    packed_rows = block_size + TRAITS + tail_rows
    left_rows = block_size + base_rows + 16
    width = 2 * row_count

    packed = pl.pallas_call(
        pack_kernel,
        out_shape=jax.ShapeDtypeStruct((packed_rows, row_count), bf16),
        in_specs=whole(3),
        out_specs=whole(1)[0],
        scratch_shapes=[pltpu.VMEM((tail_rows, row_count), f32)],
        name="pack",
    )(dosage, fold[None, :], pheno.T)

    def swap(value):
        return lax.ppermute(value, "sub", [(0, 1), (1, 0)])

    def source_of(host, turn):
        mirrored = host_count == 2 and host > first_host
        return (host - turn if mirrored else host + turn) % people_count

    order = [turn for turn in range(2, people_count - 1)] + [1, people_count - 1]
    received = {0: packed}
    for turn in order:
        received[turn] = lax.ppermute(
            packed, "people", [(source_of(host, turn), host) for host in hosts]
        )
    swapped = {turn: swap(received[turn]) for turn in [0, people_count - 1] + order[:-1]}
    chunks = []
    for turn in range(people_count):
        chunks += [received[turn], swapped[turn]]

    sizes = (
        block_size, row_count, trait_group, quarter, part_rows, first_host, host_count, people_count,
    )
    early, pheno_quarter = pl.pallas_call(
        functools.partial(early_kernel, sizes),
        out_shape=[
            jax.ShapeDtypeStruct((left_rows, block_size), f32),
            jax.ShapeDtypeStruct((16, width), bf16),
        ],
        in_specs=anywhere(4),
        out_specs=whole(2),
        scratch_shapes=[
            pltpu.VMEM((packed_rows, 2 * width), bf16),
            pltpu.VMEM((left_rows, 2 * width), bf16),
            pltpu.SemaphoreType.DMA((4,)),
        ],
        cost_estimate=pl.CostEstimate(
            flops=4 * left_rows * block_size * width,
            bytes_accessed=8 * left_rows * block_size,
            transcendentals=0,
        ),
        name="early",
    )(*chunks[:2], *chunks[-2:])
    keep, send = pl.pallas_call(
        functools.partial(fit_kernel, sizes, rows),
        out_shape=[jax.ShapeDtypeStruct((rows, people), bf16)] * 2,
        in_specs=[pl.BlockSpec(memory_space=pltpu.SMEM)] + anywhere(1 + len(chunks)),
        out_specs=whole(2),
        scratch_shapes=[
            pltpu.VMEM((packed_rows, people), bf16),
            pltpu.VMEM((left_rows, width), bf16),
            pltpu.VMEM((left_rows, block_size), f32),
            pltpu.VMEM((block_size, block_size), bf16),
            pltpu.VMEM((block_size, block_size), bf16),
            pltpu.VMEM((block_size, 8), f32),
            pltpu.VMEM(((ITERS + 1) * base_rows, block_size), f32),
            pltpu.VMEM((base_rows, block_size), f32),
            pltpu.VMEM((2 * base_rows, block_size), bf16),
            pltpu.VMEM((ITERS * base_rows, 1), f32),
            pltpu.VMEM((ITERS * base_rows, 1), f32),
            pltpu.VMEM((RIDGES * base_rows, block_size), bf16),
            pltpu.VMEM((2 * rows, people), bf16),
            pltpu.SemaphoreType.DMA((len(chunks),)),
            pltpu.SemaphoreType.DMA,
        ],
        name="fit",
    )(ridges, early, *chunks)

    pieces = pl.pallas_call(
        functools.partial(join_kernel, (first_host, host_count, people_count)),
        out_shape=[jax.ShapeDtypeStruct((rows, width), bf16)] * people_count,
        in_specs=whole(2),
        out_specs=whole(people_count),
        name="join",
    )(keep, swap(send))
    arrived = {0: pieces[0]}
    for turn in order:
        arrived[turn] = lax.ppermute(
            pieces[turn], "people", [(host, source_of(host, turn)) for host in hosts]
        )

    place = lax.axis_index("people")
    block = lax.axis_index("blocks")

    def piece_for(target):
        turn = place - first_host - target
        if host_count == 2:
            turn = jnp.where(target == 1, -turn, turn)
        turn = turn % people_count
        chosen = arrived[0]
        for other in range(1, people_count):
            chosen = jnp.where(turn == other, arrived[other], chosen)
        return chosen

    parts = [piece_for(block)]
    for turn in range(1, block_count):
        parts.append(
            lax.ppermute(
                piece_for((block + turn) % block_count),
                "blocks",
                [(source, (source + turn) % block_count) for source in range(block_count)],
            )
        )

    stat_rows = round_up(block_count * RIDGES + 1, 8)
    table_width = block_count * rows
    sums = pl.pallas_call(
        functools.partial(moment_kernel, (quarter, rows, block_count, stat_rows)),
        out_shape=jax.ShapeDtypeStruct((stat_rows, table_width), f32),
        in_specs=whole(1 + block_count),
        out_specs=whole(1)[0],
        name="moment",
    )(pheno_quarter, *parts)
    tables = [sums]
    for turn in order:
        tables.append(
            lax.ppermute(
                sums,
                "people",
                [(source, (source + turn) % people_count) for source in range(people_count)],
            )
        )
    answer = pl.pallas_call(
        functools.partial(
            second_kernel, (people, quarter, rows, block_count, stat_rows, people_count)
        ),
        out_shape=jax.ShapeDtypeStruct((RIDGES, quarter, width), f32),
        in_specs=[pl.BlockSpec(memory_space=pltpu.SMEM)] + whole(people_count + block_count),
        out_specs=whole(1)[0],
        name="second",
    )(ridges, *tables, *parts)
    return answer.transpose(1, 0, 2)


def solution(mesh):
    return jax.shard_map(
        shards,
        mesh=mesh,
        in_specs=(
            P(("groups", "people", "sub"), "blocks"),
            P(("groups", "people", "sub")),
            P(("groups", "people", "sub"), None),
            P(),
        ),
        out_specs=P(("blocks", "sub"), None, ("groups", "people")),
        check_vma=False,
    )
```
